128 devices in a mesh: rows: 4 (over y_hi, core), cols: 32 (over z, x, y_lo).
Axes of the slice: x: 4, y: 4 (y_hi: 2, y_lo: 2; y = y_hi * 2 + y_lo), z: 4, core: 2. Of those that a mesh axis runs over, the one named last changes fastest.
Arguments:
- iterate: bfloat16 [3584, 81920], P('rows', 'cols'), may hold values from -4.5 to 4.5
Outputs:
- updated: bfloat16 [3584, 81920], P('rows', 'cols')
The draws below stay inside these ranges and needn't reach their ends.
All inputs are finite; a program needn't handle non-finite values.
Results may differ from the reference program's by a relative error of at most 0.0054.
Values may be sent and summed in bfloat16 or wider, within the bound.
No kernel may reach another device: no remote copies, remote signals or barrier semaphores. Data moves between devices by JAX's collectives and lax.ppermute only.
A program may use at most 128 MiB of HBM per device.

```python
import math
import jax
import jax.numpy as jnp
from jax import lax

M = 3584
V = 81920


def draw_iterate(key, part):
    key_scale = jax.random.fold_in(key, 11)
    key_entry = jax.random.fold_in(key, 12)
    key_left = jax.random.fold_in(key, 13)
    key_right = jax.random.fold_in(key, 14)
    scales = jnp.exp(jax.random.uniform(key_scale, (M, 1), jnp.float32, minval=math.log(0.1), maxval=0.0))
    left = jax.random.normal(key_left, (M, 4), jnp.float32)
    right = jax.random.normal(key_right, (4, V), jnp.float32)
    shared = left[:, 0:1] * right[0:1, :] + left[:, 1:2] * right[1:2, :]
    shared = shared + left[:, 2:3] * right[2:3, :] + left[:, 3:4] * right[3:4, :]
    strength = math.sqrt(4.0 * 0.5 / (0.215 * M))
    noise = jax.random.normal(key_entry, (M, V), jnp.float32)
    entries = jnp.clip(strength * 0.5 * shared + noise, -4.5, 4.5)
    return (scales * entries).astype(jnp.bfloat16)


def setup_inputs(seed: int = 0) -> dict:
    arg_keys = jax.random.split(jax.random.key(seed), 2)
    return {
        "iterate": draw_iterate(jax.random.fold_in(arg_keys[1], 71), 0),
    }


linear_coef = 3.4445
cubic_coef = -4.7750
quintic_coef = 2.0315


def reference(iterate):
    values = iterate.astype(jnp.float32)
    gram = (jnp.dot(values, values.T, precision=lax.Precision.HIGHEST) / V).astype(jnp.bfloat16)
    gram_wide = gram.astype(jnp.float32)
    square = jnp.dot(gram_wide, gram_wide, precision=lax.Precision.HIGHEST)
    poly_gram = (cubic_coef * gram_wide + quintic_coef * square).astype(jnp.bfloat16)
    result = linear_coef * values + jnp.dot(poly_gram.astype(jnp.float32), values, precision=lax.Precision.HIGHEST)
    return result.astype(jnp.bfloat16)
```

```python
import jax
import jax.numpy as jnp
from jax import lax
from jax.sharding import Mesh, PartitionSpec as P

linear_coef = 3.4445
cubic_coef = -4.775
quintic_coef = 2.0315

ROWS = ("yh", "core")
COLS = ("z", "x", "yl")
PLANE = ("z", "x")
SWAP = [(0, 1), (1, 0)]

f32 = jnp.float32
bf16 = jnp.bfloat16


def swap(value, axis):
    return lax.ppermute(value, axis, SWAP)


def dot_nt(left, right):
    return lax.dot_general(left, right, (((1,), (1,)), ((), ())), preferred_element_type=f32)


def dot_tn(left, right):
    return lax.dot_general(left, right, (((0,), (0,)), ((), ())), preferred_element_type=f32)


def dot_nn(left, right):
    return jnp.dot(left, right, preferred_element_type=f32)


def ordered(mine, other, index):
    rows = mine.shape[0]
    out = jnp.zeros((2 * rows,) + mine.shape[1:], mine.dtype)
    out = lax.dynamic_update_slice_in_dim(out, mine, index * rows, 0)
    return lax.dynamic_update_slice_in_dim(out, other, (1 - index) * rows, 0)


def plane_sum(partial):
    count = lax.axis_size("z") * lax.axis_size("x")
    sent = partial.astype(bf16)
    got = lax.all_to_all(sent, PLANE, 0, 0, tiled=True)
    got = got.reshape((count, sent.shape[0] // count, sent.shape[1]))
    return jnp.sum(got.astype(f32), axis=0)


def on_device(x):
    h = lax.axis_index("yh")
    k = lax.axis_index("core")
    rows, width = x.shape
    half = width // 2
    vocab = width * lax.axis_size("z") * lax.axis_size("x") * lax.axis_size("yl")

    send_first = lax.dynamic_slice_in_dim(x, (1 - h) * half, half, 1)
    keep_first = lax.dynamic_slice_in_dim(x, h * half, half, 1)
    x_core = swap(x, "core")
    far_first = swap(send_first, "yh")
    pair = ordered(x, x_core, k)

    near_part = dot_nt(x, pair)
    near_sum = plane_sum(near_part)
    near_sum = near_sum + swap(near_sum, "yl")
    near_mine = (near_sum / vocab).astype(bf16)

    far_first_core = swap(far_first, "core")
    far_pair_first = ordered(far_first, far_first_core, k)
    pair_half = lax.dynamic_slice_in_dim(pair, h * half, half, 1)
    left = jnp.where(h == 0, keep_first, far_first)
    right = jnp.where(h == 0, far_pair_first, pair_half)
    cross_part = dot_nt(left, right)

    keep_late, _ = lax.optimization_barrier((keep_first, far_first))
    far_second = swap(keep_late, "yh")
    far_second_core = swap(far_second, "core")
    far_pair_second = ordered(far_second, far_second_core, k)

    near_other = swap(near_mine, "yh")
    s_own = lax.all_gather(near_mine, PLANE, axis=0, tiled=True)
    s_oth = lax.all_gather(near_other, PLANE, axis=0, tiled=True)
    s_own_full = ordered(s_own, swap(s_own, "core"), k)
    s_oth_full = ordered(s_oth, swap(s_oth, "core"), k)

    cross_sum = plane_sum(cross_part)
    cross_sum = cross_sum + swap(cross_sum, "yl")
    cross_sum = cross_sum + swap(cross_sum, "yh")
    cross_mine = (cross_sum / vocab).astype(bf16)
    c_mine = lax.all_gather(cross_mine, PLANE, axis=0, tiled=True)
    c_full = ordered(c_mine, swap(c_mine, "core"), k)

    def poly(gram, square):
        return (cubic_coef * gram.astype(f32) + quintic_coef * square).astype(bf16)

    def low(s_mine, s_full, so_full, c):
        ck = lax.dynamic_slice_in_dim(c, k * rows, rows, 0)
        own = poly(s_mine, dot_nn(s_mine, s_full) + dot_nt(ck, c))
        oth = poly(ck, dot_nn(s_mine, c) + dot_nn(ck, so_full))
        return own, oth

    def high(s_mine, s_full, so_full, c):
        ck = lax.dynamic_slice_in_dim(c, k * rows, rows, 1)
        own = poly(s_mine, dot_nn(s_mine, s_full) + dot_tn(ck, c))
        oth = poly(ck.T, dot_nt(s_mine, c) + dot_tn(ck, so_full))
        return own, oth

    p_own, p_oth = lax.cond(h == 0, low, high, s_own, s_own_full, s_oth_full, c_full)

    far = jnp.zeros((2 * rows, width), x.dtype)
    far = lax.dynamic_update_slice_in_dim(far, far_pair_first, h * half, 1)
    far = lax.dynamic_update_slice_in_dim(far, far_pair_second, (1 - h) * half, 1)
    mixed = linear_coef * x.astype(f32) + dot_nn(p_own, pair) + dot_nn(p_oth, far)
    return mixed.astype(bf16)


def solution(mesh):
    fine = Mesh(mesh.devices.reshape(2, 2, 4, 4, 2), ROWS + COLS)
    return jax.shard_map(
        on_device,
        mesh=fine,
        in_specs=(P(ROWS, COLS),),
        out_specs=P(ROWS, COLS),
        check_vma=False,
    )
```
